256 devices in a mesh: seq: 16 (over x_hi, y, core), tp: 16 (over x_lo, z).
Axes of the slice: x: 4 (x_hi: 2, x_lo: 2; x = x_hi * 2 + x_lo), y: 4, z: 8, core: 2. Of those that a mesh axis runs over, the one named last changes fastest.
Arguments:
- hidden: bfloat16 [8192, 3584], P('seq', 'tp'), may hold values from -6 to 6
- modality: int32 [8192], P('seq'), may hold values from 0 to 2, as said below
- segment_bounds: int32 [6], replicated, may hold values from 0 to 8192, as said below
- block_mask: int32 [64, 64], replicated, may hold values from 0 to 1, as said below
- norm_gain: float32 [2, 2, 3584], replicated, may hold values from 0.1 to 1.9
- query_weight: bfloat16 [2, 3584, 2048], P(None, None, 'tp'), may hold values from -1 to 1
- keys_values: bfloat16 [2, 3584, 1024], P(None, None, 'tp'), may hold values from -1 to 1
- output_weight: bfloat16 [2, 2048, 3584], P(None, 'tp'), may hold values from -0.375 to 0.375
- gate_weight: bfloat16 [7168, 10240], P('seq', 'tp'), may hold values from -0.09375 to 0.09375
- up_weight: bfloat16 [7168, 10240], P('seq', 'tp'), may hold values from -0.09375 to 0.09375
- down_weight: bfloat16 [7168, 10240], P('seq', 'tp'), may hold values from -0.0625 to 0.0625
Outputs:
- layer_output: bfloat16 [8192, 3584], P('seq', 'tp')
The draws below stay inside these ranges and needn't reach their ends.
Inputs may be any that keep to these rules, and one draw needn't show every extreme that they name: `modality`: rows below 4096 carry 0 (text) or 1 (understanding image), constant over aligned runs of 32 rows; all other rows carry 2 (generation image). `segment_bounds`: strictly increasing; the first entry is 0 and the last 8192. `block_mask`: every diagonal entry is 1.
All inputs are finite; a program needn't handle non-finite values.
Results may differ from the reference program's by a relative error of at most 0.02.
The reference program's roundings to bfloat16 on the way count: a program that leaves them out, or rounds other values in their place, can miss the bound.
Values may be sent and summed in bfloat16 or wider, within the bound.
No kernel may reach another device: no remote copies, remote signals or barrier semaphores. Data moves between devices by JAX's collectives and lax.ppermute only.
A program may use at most 128 MiB of HBM per device.

```python
import math
import jax
import jax.numpy as jnp
from jax import lax

D = 3584
FF = 10240
HEADS = 16
KVH = 4
HD = 128
BLOCK = 128
SEGS = 5
TOKENS = 8192
NB = 64
N_TP = 16


def projection_draw(key, salt, count):
    own_key = jax.random.fold_in(key, salt)
    base = jnp.clip(jax.random.normal(own_key, (2, D, count), jnp.float32), -6.0, 6.0) * D ** (-0.5)
    return base


def draw_hidden(key, part):
    own_key = jax.random.fold_in(key, 202)
    rows = jnp.clip(jax.random.normal(own_key, (TOKENS, D), jnp.float32), -6.0, 6.0)
    return rows.astype(jnp.bfloat16)


def draw_query_weight(key, part):
    return projection_draw(key, 101, HEADS * HD).astype(jnp.bfloat16)


def draw_keys_values(key, part):
    count = 2 * KVH * HD
    return projection_draw(key, 303, count).astype(jnp.bfloat16)


def draw_modality(key, part):
    half_rows = TOKENS // 2
    run_flags = jax.random.randint(key, (half_rows // 32,), 0, 2).astype(jnp.int32)
    leading = jnp.repeat(run_flags, 32)
    trailing = jnp.full((TOKENS - half_rows,), 2, jnp.int32)
    return jnp.concatenate([leading, trailing]).astype(jnp.int32)


def draw_segment_bounds(key, part):
    first_key = jax.random.fold_in(key, 11)
    rest_key = jax.random.fold_in(key, 12)
    spread = TOKENS // 16
    long_end = 3 * TOKENS // 4 + jax.random.randint(first_key, (), -spread, spread + 1).astype(jnp.int32)
    tail_length = TOKENS - long_end
    tail_count = SEGS - 1
    steps_after = jnp.arange(1, tail_count, dtype=jnp.int32)
    base_bounds = long_end + tail_length * steps_after // tail_count
    jitter = TOKENS // (16 * tail_count)
    offsets = jax.random.randint(rest_key, (tail_count - 1,), -jitter, jitter + 1).astype(jnp.int32)
    return jnp.concatenate([jnp.zeros((1,), jnp.int32), long_end.reshape(1), (base_bounds + offsets).astype(jnp.int32), jnp.full((1,), TOKENS, jnp.int32)]).astype(jnp.int32)


def draw_block_mask(key, part):
    coin_flips = jax.random.randint(key, (NB, NB), 0, 4)
    diagonal = jnp.eye(NB, dtype=jnp.int32)
    return jnp.maximum((coin_flips > 0).astype(jnp.int32), diagonal)


def levels(key, dims, cuts, least, largest):
    loudness, own = 1.0, jax.random.fold_in(key, 6)
    for axis_at, blocks in cuts:
        heights = jnp.exp(jax.random.uniform(jax.random.fold_in(own, axis_at), (blocks,), jnp.float32, least / len(cuts), largest / len(cuts)))
        loudness = loudness * jnp.repeat(heights, dims[axis_at] // blocks).reshape([-1 if axis == axis_at else 1 for axis in range(len(dims))])
    return loudness


def centred(stream_key, extent, width, limit, split=(), held_as=jnp.bfloat16):
    gain = levels(stream_key, extent, split, -0.22, 0.18) if split else 1.0
    entries = jax.random.normal(stream_key, extent, jnp.float32) * width * gain
    return jnp.minimum(jnp.maximum(entries, -limit), limit).astype(held_as)


def setup_inputs(seed: int = 0) -> dict:
    arg_keys = jax.random.split(jax.random.key(seed), 12)
    hidden = draw_hidden(jax.random.fold_in(arg_keys[11], 71), 0)
    modality = draw_modality(jax.random.fold_in(arg_keys[11], 71), 0)
    segment_bounds = draw_segment_bounds(jax.random.fold_in(arg_keys[11], 71), 0)
    block_mask = draw_block_mask(jax.random.fold_in(arg_keys[11], 71), 0)
    norm_gain = jnp.clip(1.0 + 0.18 * jax.random.normal(arg_keys[4], (2, 2, D), jnp.float32), 0.1, 1.9)
    query_weight = draw_query_weight(jax.random.fold_in(arg_keys[11], 71), 0)
    keys_values = draw_keys_values(jax.random.fold_in(arg_keys[11], 71), 0)
    output_weight = centred(arg_keys[7], (2, HEADS * HD, D), (HEADS * HD // 8) ** -0.5, 0.375, ((1, 16),))
    gate_weight = centred(arg_keys[8], (2 * D, FF), D ** -0.5, 0.09375, ((0, 16), (1, 16)))
    up_weight = centred(arg_keys[9], (2 * D, FF), D ** -0.5, 0.09375, ((0, 16), (1, 16)))
    down_weight = centred(arg_keys[10], (2 * D, FF), FF ** -0.5, 0.0625, ((0, 16), (1, 16)))
    return {"hidden": hidden, "modality": modality, "segment_bounds": segment_bounds, "block_mask": block_mask, "norm_gain": norm_gain, "query_weight": query_weight, "keys_values": keys_values, "output_weight": output_weight, "gate_weight": gate_weight, "up_weight": up_weight, "down_weight": down_weight}


theta_base = 1000000.0
epsilon = 1e-06
masked_score = -1e+30

def normalize(values, gain_row):
    widened = values.astype(jnp.float32)
    mean_square = lax.optimization_barrier(jnp.mean(widened * widened, axis=-1, keepdims=True))
    return (widened * lax.rsqrt(mean_square + epsilon) * gain_row).astype(jnp.bfloat16)

def rotary(values, offsets):
    half_dim = values.shape[-1] // 2
    frequency = theta_base ** (-2.0 * jnp.arange(half_dim, dtype=jnp.float32) / values.shape[-1])
    angles = offsets.astype(jnp.float32)[:, None] * frequency[None, :]
    cosine = jnp.cos(angles)[:, None, :]
    sine_part = jnp.sin(angles)[:, None, :]
    leading = values[..., :half_dim]
    trailing = values[..., half_dim:]
    return jnp.concatenate([leading * cosine - trailing * sine_part, trailing * cosine + leading * sine_part], axis=-1)

def segment_info(positions, segment_bounds):
    openings = segment_bounds[:-1]
    inside = positions[:, None] >= openings[None, :]
    segment_ids = lax.optimization_barrier(jnp.sum(inside.astype(jnp.int32), axis=1))
    opening = lax.optimization_barrier(jnp.max(jnp.where(inside, openings[None, :], 0), axis=1))
    return (segment_ids, positions - opening)

def sliced_sum(left_side, right_side, piece_count):
    piece_width = left_side.shape[1] // piece_count

    def accumulate(running, piece_number):
        left_piece = lax.dynamic_slice_in_dim(left_side, piece_number * piece_width, piece_width, 1)
        right_piece = lax.dynamic_slice_in_dim(right_side, piece_number * piece_width, piece_width, 0)
        rounded = lax.optimization_barrier(jnp.dot(left_piece, right_piece, preferred_element_type=jnp.float32).astype(jnp.bfloat16))
        return (running + rounded.astype(jnp.float32), None)
    initial = jnp.zeros((left_side.shape[0], right_side.shape[1]), jnp.float32)
    return lax.scan(accumulate, initial, jnp.arange(piece_count, dtype=jnp.int32))[0]

def reference(hidden, modality, segment_bounds, block_mask, norm_gain, query_weight, keys_values, output_weight, gate_weight, up_weight, down_weight):
    half_rows = TOKENS // 2
    positions = jnp.arange(TOKENS, dtype=jnp.int32)
    segment_ids, offsets = segment_info(positions, segment_bounds)
    query_parts, key_parts, value_parts = ([], [], [])
    for weight_set in range(2):
        first_row = weight_set * half_rows
        normed = normalize(hidden[first_row:first_row + half_rows], norm_gain[weight_set, 0])
        query_block = jnp.dot(normed, query_weight[weight_set], preferred_element_type=jnp.float32).reshape(half_rows, HEADS, HD)
        query_parts.append(rotary(query_block, offsets[first_row:first_row + half_rows]).astype(jnp.bfloat16))
        projected = jnp.dot(normed, keys_values[weight_set], preferred_element_type=jnp.float32).astype(jnp.bfloat16)
        raw_keys = projected[:, :KVH * HD].astype(jnp.float32).reshape(half_rows, KVH, HD)
        key_parts.append(rotary(raw_keys, offsets[first_row:first_row + half_rows]).astype(jnp.bfloat16))
        value_parts.append(projected[:, KVH * HD:].reshape(half_rows, KVH, HD))
    queries = jnp.concatenate(query_parts, 0)
    keys_all = jnp.concatenate(key_parts, 0)
    values_all = jnp.concatenate(value_parts, 0)
    group_size = HEADS // KVH
    query_step = math.gcd(TOKENS, 512)
    score_scale = HD ** (-0.5)
    key_blocks = positions // BLOCK

    def one_head(head_number):
        query_head = lax.dynamic_index_in_dim(queries, head_number, 1, keepdims=False)
        key_head = lax.dynamic_index_in_dim(keys_all, head_number // group_size, 1, keepdims=False)
        value_head = lax.dynamic_index_in_dim(values_all, head_number // group_size, 1, keepdims=False)

        def one_block(block_start):
            query_rows = lax.dynamic_slice_in_dim(query_head, block_start, query_step, 0)
            query_positions = block_start + jnp.arange(query_step, dtype=jnp.int32)
            query_segments = lax.dynamic_slice_in_dim(segment_ids, block_start, query_step, 0)
            query_modes = lax.dynamic_slice_in_dim(modality, block_start, query_step, 0)
            coarse = block_mask[(query_positions // BLOCK)[:, None], key_blocks[None, :]] == 1
            mutual = (query_modes[:, None] > 0) & (query_modes[:, None] == modality[None, :])
            allowed = coarse & (query_segments[:, None] == segment_ids[None, :]) & ((positions[None, :] <= query_positions[:, None]) | mutual)
            scores = jnp.dot(query_rows, key_head.T, preferred_element_type=jnp.float32) * score_scale
            scores = jnp.where(allowed, scores, masked_score)
            row_peak = lax.optimization_barrier(jnp.max(scores, axis=1, keepdims=True))
            exponent = jnp.where(allowed, jnp.exp(scores - row_peak), 0.0)
            mixed = jnp.dot(exponent.astype(jnp.bfloat16), value_head, preferred_element_type=jnp.float32)
            return (mixed / lax.optimization_barrier(jnp.sum(exponent, axis=1, keepdims=True))).astype(jnp.bfloat16)
        starts = jnp.arange(TOKENS // query_step, dtype=jnp.int32) * query_step
        return lax.map(one_block, starts).reshape(TOKENS, HD)
    attended = lax.map(one_head, jnp.arange(HEADS, dtype=jnp.int32))
    attended = attended.transpose(1, 0, 2).reshape(TOKENS, HEADS * HD)
    outputs = []
    for weight_set in range(2):
        first_row = weight_set * half_rows
        attention_sum = sliced_sum(attended[first_row:first_row + half_rows], output_weight[weight_set], N_TP)
        residual = (hidden[first_row:first_row + half_rows].astype(jnp.float32) + attention_sum).astype(jnp.bfloat16)
        second_normed = normalize(residual, norm_gain[weight_set, 1])
        gate_values = jnp.dot(second_normed, gate_weight[weight_set * D:(weight_set + 1) * D], preferred_element_type=jnp.float32)
        up_values = jnp.dot(second_normed, up_weight[weight_set * D:(weight_set + 1) * D], preferred_element_type=jnp.float32)
        active = (jax.nn.silu(gate_values) * up_values).astype(jnp.bfloat16)
        down_sum = sliced_sum(active, down_weight[weight_set * D:(weight_set + 1) * D].T, N_TP)
        outputs.append((residual.astype(jnp.float32) + down_sum).astype(jnp.bfloat16))
    return jnp.concatenate(outputs, 0)
```

```python
import functools
import jax
import jax.numpy as jnp
from jax import lax
from jax.experimental import pallas as pl
from jax.experimental.pallas import tpu as pltpu
from jax.sharding import PartitionSpec as P

HEADS = 16
KVH = 4
HD = 128
BLOCK = 128
RUN = 32
Y_COUNT = 4
Z_COUNT = 8

theta_base = 1000000.0
epsilon = 1e-06
masked_score = -1e30
lowest_peak = -1e29
far = 1 << 29


vmem = pl.BlockSpec(memory_space=pltpu.VMEM)
smem = pl.BlockSpec(memory_space=pltpu.SMEM)
anywhere = pl.BlockSpec(memory_space=pl.ANY)

TREE = (
    ((0, 0), (0, 0), (0, 0)),
    ((0, 7), (0, 1), (0, 7)),
    ((0, 6), (0, 2), (0, 1)),
    ((0, 5), (1, 1), (0, 6)),
    ((1, 6), (1, 2), (0, 4)),
)
PLACES = tuple((flip, offset) for flip in range(2) for offset in range(Z_COUNT))


def tp_send(block, flip, step):
    route = []
    for source in range(2 * Z_COUNT):
        x, z = divmod(source, Z_COUNT)
        route.append((source, (x ^ flip) * Z_COUNT + (z + step) % Z_COUNT))
    return lax.ppermute(block, "tp", route)


def moves_of(step):
    up, down, across = step
    return (
        (up, (up[0], (up[1] - 1) % Z_COUNT), 0, 1),
        (down, (down[0], (down[1] + 1) % Z_COUNT), 0, -1),
        (across, (across[0] ^ 1, across[1]), 1, 0),
    )


def gather_tp(own):
    held = {(0, 0): own}
    for step in TREE:
        arrived = {}
        for sent, place, flip, stride in moves_of(step):
            arrived[place] = tp_send(held[sent], flip, stride)
        held.update(arrived)
    return [held[place] for place in PLACES]


def scatter_tp(terms):
    held = dict(zip(PLACES, terms))
    for step in reversed(TREE):
        arrived = []
        for sent, place, flip, stride in moves_of(step):
            arrived.append((sent, tp_send(held[place], flip, -stride)))
        for sent, value in arrived:
            total = held[sent].astype(jnp.float32) + value.astype(jnp.float32)
            held[sent] = total.astype(jnp.bfloat16)
    return held[(0, 0)]


def seq_route(target):
    route = []
    for source in range(4 * Y_COUNT):
        half, y, core = source // (2 * Y_COUNT), source // 2 % Y_COUNT, source % 2
        place = target(half, y, core)
        if place is not None:
            route.append((source, (place[0] * Y_COUNT + place[1] % Y_COUNT) * 2 + place[2]))
    return route


def y_send(block, stride):
    return lax.ppermute(block, "seq", seq_route(lambda half, y, core: (half, y + stride, core)))


def core_send(block):
    return lax.ppermute(block, "seq", seq_route(lambda half, y, core: (half, y, 1 - core)))


def half_send(block):
    return lax.ppermute(
        block, "seq", seq_route(lambda half, y, core: (1, y, core) if half == 0 else None)
    )


def tied(block, *others):
    return lax.optimization_barrier((block,) + others)[0]


def wide(row, width):
    return jnp.concatenate([row] * (width // row.shape[1]), axis=1)


def store_normed(places, pieces, gain_ref, normed_ref):
    depth, rows = pieces[0].shape
    total = jnp.zeros((1, rows), jnp.float32)
    for piece in pieces:
        value = piece[...].astype(jnp.float32)
        total += jnp.sum(value * value, axis=0, keepdims=True)
    inverse = lax.rsqrt(total / (depth * len(pieces)) + epsilon)
    for index, piece in enumerate(pieces):
        at = pl.multiple_of(places[index] * depth, depth)
        gain = wide(gain_ref[pl.ds(at, depth), :], rows)
        value = piece[...].astype(jnp.float32) * inverse * gain
        normed_ref[pl.ds(at, depth), :] = value.astype(jnp.bfloat16)


def turn(top, bottom, cosine, sine):
    return jnp.concatenate([top * cosine - bottom * sine, bottom * cosine + top * sine], axis=0)


def project_kernel(places, gain_ref, weight_ref, cosine_ref, sine_ref, *rest):
    pieces, (query_ref, pair_ref, normed_ref) = rest[:16], rest[16:]
    store_normed(places, pieces, gain_ref, normed_ref)
    result = jnp.dot(weight_ref[...], normed_ref[...], preferred_element_type=jnp.float32)
    half = HD // 2
    turned = turn(result[:half], result[half:HD], cosine_ref[...], sine_ref[...])
    query_ref[...] = turned.astype(jnp.bfloat16)
    pair_ref[...] = result[HD:].astype(jnp.bfloat16)


def project(places, gain, weight, cosine, sine, pieces):
    depth, rows = pieces[0].shape
    count = weight.shape[0]
    return pl.pallas_call(
        project_kernel,
        out_shape=(
            jax.ShapeDtypeStruct((HD, rows), jnp.bfloat16),
            jax.ShapeDtypeStruct((count - HD, rows), jnp.bfloat16),
        ),
        in_specs=[smem] + [vmem] * (4 + len(pieces)),
        out_specs=(vmem, vmem),
        scratch_shapes=[pltpu.VMEM((depth * len(pieces), rows), jnp.bfloat16)],
        name="project",
    )(places, gain, weight, cosine, sine, *pieces)


def pack_kernel(member_ref, cosine_ref, sine_ref, flag_ref, *rest):
    received, out_ref = rest[:4], rest[4]
    member = member_ref[0]

    def block(number):
        index = lax.rem(member - number + 4, 4)
        value = received[3][...]
        for candidate in range(3):
            value = jnp.where(index == candidate, received[candidate][...], value)
        return value

    keys = turn(
        block(0).astype(jnp.float32),
        block(1).astype(jnp.float32),
        cosine_ref[...],
        sine_ref[...],
    )
    keys = keys.T.astype(jnp.bfloat16)
    values = jnp.concatenate([block(2), block(3)], axis=0)
    part = out_ref.shape[0] // 2
    for index in range(2):
        base = index * part
        out_ref[base : base + 256, :] = keys[256 * index : 256 * index + 256]
        for column in range(2):
            start = 256 * index + HD * column
            row = base + 256 + HD * column
            out_ref[row : row + HD, :] = values[:, start : start + HD]
        out_ref[base + 512 : base + 528, :] = flag_ref[16 * index : 16 * index + 16, :]


def pack(member, cosine, sine, flags, received):
    return pl.pallas_call(
        pack_kernel,
        out_shape=jax.ShapeDtypeStruct((1056, HD), jnp.bfloat16),
        in_specs=[smem] + [vmem] * 7,
        out_specs=vmem,
        name="pack",
    )(member, cosine, sine, flags, *received)


def attend_kernel(count, last, places, live, query_ref, low_ref, limit_ref, *rest):
    pieces = rest[:count]
    before, after = rest[count : count + 3], rest[count + 3 : count + 6]
    peak_ref, sum_ref, mixed_ref = after
    for source, target in zip(before, after):
        target[...] = source[...]
    rows = query_ref.shape[1]
    scale = HD ** (-0.5) * 1.4426950408889634
    for index in range(count):
        for part in range(2):
            place = places[index]

            def step(piece=pieces[index], place=place, part=part):
                base = 528 * part
                raw = jnp.dot(
                    piece[base : base + 256, :], query_ref[...], preferred_element_type=jnp.float32
                )
                first = place * 512 + part * 256
                flags = piece[base + 512 : base + 528, :].astype(jnp.float32)
                plain, mutual = limit_ref[0:1, :], limit_ref[1:2, :]
                scores = []
                for run in range(256 // RUN):
                    low = low_ref[pl.ds(place * 4 + part * 2 + run * RUN // BLOCK, 1), :]
                    flag = wide(flags[run : run + 1, :], rows)
                    high = jnp.where(flag > 0.5, mutual, plain)
                    keys = lax.broadcasted_iota(jnp.int32, (RUN, rows), 0) + (first + run * RUN)
                    allowed = (keys >= low) & (keys <= high)
                    score = raw[run * RUN : run * RUN + RUN, :] * scale
                    scores.append(jnp.where(allowed, score, masked_score))
                scores = jnp.concatenate(scores, axis=0)
                old = peak_ref[...]
                new = jnp.maximum(old, jnp.max(scores, axis=0, keepdims=True))
                expo = jnp.exp2(scores - new)
                fading = jnp.exp2(old - new)
                peak_ref[...] = new
                sum_ref[...] = sum_ref[...] * fading + jnp.sum(expo, axis=0, keepdims=True)
                values = jnp.concatenate(
                    [piece[base + 256 : base + 384, :], piece[base + 384 : base + 512, :]], axis=1
                )
                mixed_ref[...] = mixed_ref[...] * fading + jnp.dot(
                    values, expo.astype(jnp.bfloat16), preferred_element_type=jnp.float32
                )

            pl.when(live[place * 2 + part] > 0)(step)
    if last:
        rest[-1][...] = (mixed_ref[...] / sum_ref[...]).astype(jnp.bfloat16)


def attend(places, live, query, low, limit, pieces, running, last):
    rows = query.shape[1]
    shapes = [
        jax.ShapeDtypeStruct((1, rows), jnp.float32),
        jax.ShapeDtypeStruct((1, rows), jnp.float32),
        jax.ShapeDtypeStruct((HD, rows), jnp.float32),
    ]
    if last:
        shapes.append(jax.ShapeDtypeStruct((HD, rows), jnp.bfloat16))
    count = len(pieces)
    return pl.pallas_call(
        functools.partial(attend_kernel, count, last),
        out_shape=shapes,
        in_specs=[smem, smem] + [vmem] * (6 + count),
        out_specs=[vmem] * len(shapes),
        cost_estimate=pl.CostEstimate(
            flops=4 * HD * rows * 512 * count, bytes_accessed=300000 * count, transcendentals=rows * 512 * count
        ),
        name="attend",
    )(places, live, query, low, limit, *pieces, *running)


def terms_kernel(places, weight_ref, attended_ref, *outs):
    depth = outs[0].shape[0]
    for index, out in enumerate(outs):
        at = pl.multiple_of(places[index] * depth, depth)
        result = jnp.dot(
            weight_ref[pl.ds(at, depth), :], attended_ref[...], preferred_element_type=jnp.float32
        )
        out[...] = result.astype(jnp.bfloat16)


def head_terms(places, weight, attended):
    rows = attended.shape[1]
    depth = weight.shape[0] // 16
    return pl.pallas_call(
        terms_kernel,
        out_shape=[jax.ShapeDtypeStruct((depth, rows), jnp.bfloat16)] * 16,
        in_specs=[smem, vmem, vmem],
        out_specs=[vmem] * 16,
        name="terms",
    )(places, weight, attended)


def feed_kernel(places, shards, gain_ref, *rest):
    pieces, weights, outs = rest[:16], rest[16:24], rest[24:40]
    normed_ref, gate_ref, up_ref, down_ref, arrived = rest[40:]
    depth = weights[0].shape[0] // 3
    targets = (gate_ref, up_ref, down_ref)
    copies = []
    for kind, target in enumerate(targets):
        for index, weight in enumerate(weights):
            at = pl.multiple_of(shards[index] * depth, depth)
            copy = pltpu.make_async_copy(
                weight.at[pl.ds(kind * depth, depth), :],
                target.at[pl.ds(at, depth), :],
                arrived.at[kind, index],
            )
            copy.start()
            copies.append(copy)
    store_normed(places, pieces, gain_ref, normed_ref)
    for copy in copies[:16]:
        copy.wait()
    across = (((0,), (0,)), ((), ()))
    gate = lax.dot_general(normed_ref[...], gate_ref[...], across, preferred_element_type=jnp.float32)
    up = lax.dot_general(normed_ref[...], up_ref[...], across, preferred_element_type=jnp.float32)
    active = (gate / (1.0 + jnp.exp(-gate)) * up).T.astype(jnp.bfloat16)
    for copy in copies[16:]:
        copy.wait()
    share = outs[0].shape[0]
    for index, out in enumerate(outs):
        at = pl.multiple_of(places[index] * share, share)
        result = jnp.dot(down_ref[pl.ds(at, share), :], active, preferred_element_type=jnp.float32)
        out[...] = result.astype(jnp.bfloat16)


def feed(places, shards, gain, pieces, weights):
    depth, rows = pieces[0].shape
    full, hidden_units = depth * 16, weights[0].shape[1]
    return pl.pallas_call(
        feed_kernel,
        out_shape=[jax.ShapeDtypeStruct((depth, rows), jnp.bfloat16)] * 16,
        in_specs=[smem, smem] + [vmem] * 17 + [anywhere] * 8,
        out_specs=[vmem] * 16,
        scratch_shapes=[pltpu.VMEM((full, rows), jnp.bfloat16)]
        + [pltpu.VMEM((full, hidden_units), jnp.bfloat16)] * 3
        + [pltpu.SemaphoreType.DMA((3, 8))],
        name="feed",
    )(places, shards, gain, *pieces, *weights)


def body(
    hidden,
    modality,
    segment_bounds,
    block_mask,
    norm_gain,
    query_weight,
    keys_values,
    output_weight,
    gate_weight,
    up_weight,
    down_weight,
):
    seq_index = lax.axis_index("seq")
    tp_index = lax.axis_index("tp")
    rows = hidden.shape[0]
    tokens = rows * 16
    half = seq_index // (2 * Y_COUNT)
    y, core = seq_index // 2 % Y_COUNT, seq_index % 2
    own_hidden = hidden.T

    places = jnp.stack(
        [
            (tp_index // Z_COUNT ^ flip) * Z_COUNT + (tp_index + offset) % Z_COUNT
            for flip, offset in PLACES
        ]
    ).astype(jnp.int32)
    shifts = (0, -1, 1, 2)
    same_core = jnp.stack([(y + shift) % Y_COUNT * 2 + core for shift in shifts])
    other_core = jnp.stack([(y + shift) % Y_COUNT * 2 + 1 - core for shift in shifts])
    shards = jnp.concatenate([same_core, other_core]).astype(jnp.int32)
    own_places = shards + half * 2 * Y_COUNT

    weight_stack = jnp.concatenate([gate_weight, up_weight, down_weight], axis=0)
    hidden_pieces = gather_tp(own_hidden)
    weight_near = [weight_stack, y_send(weight_stack, 1), y_send(weight_stack, -1)]

    positions = seq_index * rows + jnp.arange(rows, dtype=jnp.int32)
    openings, closings = segment_bounds[:-1], segment_bounds[1:]
    inside = positions[:, None] >= openings[None, :]
    opening = jnp.max(jnp.where(inside, openings[None, :], 0), axis=1)
    closing = jnp.min(jnp.where(positions[:, None] < closings[None, :], closings[None, :], tokens), axis=1)
    frequency = theta_base ** (-2.0 * jnp.arange(HD // 2, dtype=jnp.float32) / HD)
    angles = frequency[:, None] * (positions - opening).astype(jnp.float32)[None, :]
    cosine, sine = jnp.cos(angles), jnp.sin(angles)
    plain = jnp.where(half == 1, closing - 1, positions)
    mutual = jnp.where(modality == 1, closing - 1, plain)
    limit = jnp.stack([plain, mutual])
    block_rows = rows // BLOCK
    mask_rows = lax.dynamic_slice_in_dim(block_mask, seq_index * block_rows, block_rows, 0)
    coarse = jnp.repeat(mask_rows.T, BLOCK, axis=1) == 1
    low = jnp.where(coarse, opening[None, :], far)
    starts = jnp.arange(block_mask.shape[1], dtype=jnp.int32)[:, None] * BLOCK
    touched = (low <= starts + (BLOCK - 1)) & (mutual[None, :] >= starts)
    live = jnp.any(touched.reshape(-1, 2 * rows), axis=1).astype(jnp.int32)
    flags = (modality.reshape(2, rows // RUN // 2, RUN)[:, :, 0] == 1).astype(jnp.bfloat16)
    flags = jnp.pad(flags, ((0, 0), (0, 8)))
    flags = jnp.broadcast_to(flags.reshape(32, 1), (32, HD))
    gains = lax.dynamic_index_in_dim(norm_gain, half, 0, keepdims=False)
    gains = jnp.broadcast_to(gains[:, :, None], gains.shape + (HD,))
    local_weight = jnp.concatenate(
        [
            lax.dynamic_index_in_dim(query_weight, half, 0, keepdims=False).T,
            lax.dynamic_index_in_dim(keys_values, half, 0, keepdims=False).T,
        ],
        axis=0,
    )
    local_output = lax.dynamic_index_in_dim(output_weight, half, 0, keepdims=False).T

    query, pair = project(places, gains[0], local_weight, cosine, sine, hidden_pieces)

    group = KVH
    received = []
    for shift in range(4):
        route = []
        for head in range(KVH):
            for number in range(4):
                source = number // 2 * Z_COUNT + 2 * head + number % 2
                route.append((source, group * head + (number + shift) % 4))
        received.append(lax.ppermute(pair, "tp", route))
    member = (tp_index % 4).astype(jnp.int32).reshape(1)
    packed = pack(member, cosine, sine, flags, received)

    near = [packed, y_send(packed, 1), y_send(packed, -1), y_send(packed, 2)]
    lower = half_send(packed)
    other = [core_send(piece) for piece in near]
    lower_near = [lower, y_send(lower, 1), y_send(lower, -1), y_send(lower, 2)]
    lower_other = [core_send(piece) for piece in lower_near]
    weight_far = y_send(tied(weight_stack, lower_near[3]), 2)

    running = (
        jnp.full((1, rows), lowest_peak, jnp.float32),
        jnp.zeros((1, rows), jnp.float32),
        jnp.zeros((HD, rows), jnp.float32),
    )
    upper_live = live * half
    running = attend(own_places[:4], live, query, low, limit, near, running, False)
    running = attend(own_places[4:], live, query, low, limit, other, running, False)
    running = attend(shards[:4], upper_live, query, low, limit, lower_near, running, False)
    attended = attend(shards[4:], upper_live, query, low, limit, lower_other, running, True)[-1]

    terms = head_terms(places, local_output, attended)
    share = scatter_tp(terms)
    residual = (own_hidden.astype(jnp.float32) + share.astype(jnp.float32)).astype(jnp.bfloat16)
    pieces = gather_tp(residual)

    weights = weight_near + [weight_far]
    weights = weights + [core_send(weight) for weight in weights]
    down_terms = feed(places, shards, gains[1], pieces, weights)
    down_share = scatter_tp(down_terms)
    result = residual.astype(jnp.float32) + down_share.astype(jnp.float32)
    return result.astype(jnp.bfloat16).T


def solution(mesh):
    placed = (
        P("seq", "tp"),
        P("seq"),
        P(),
        P(),
        P(),
        P(None, None, "tp"),
        P(None, None, "tp"),
        P(None, "tp", None),
        P("seq", "tp"),
        P("seq", "tp"),
        P("seq", "tp"),
    )
    return jax.shard_map(
        body, mesh=mesh, in_specs=placed, out_specs=P("seq", "tp"), check_vma=False
    )
```
